512 devices in a mesh: seq: 16 (over z), blk: 32 (over y, x, core).
Axes of the slice: x: 4, y: 4, z: 16, core: 2. Of those that a mesh axis runs over, the one named last changes fastest.
Arguments:
- train_acts: bfloat16 [65536, 4096], P(('seq', 'blk')), may hold values from -6 to 6
- train_grads: bfloat16 [65536, 14336], P(('seq', 'blk')), may hold values from -0.0234375 to 0.0234375
- block_table: int32 [32, 2], replicated, may hold values from 0 to 55, as said below
- seq_lengths: int32 [64], replicated, may hold values from 256 to 1024, as said below
- query_acts: bfloat16 [32, 256, 256], P('blk', 'seq'), may hold values from -6 to 6
- query_grads: bfloat16 [32, 256, 256], P('blk', 'seq'), may hold values from -6 to 6
- basis_acts: bfloat16 [32, 256, 256], P('blk', 'seq'), may hold values from -0.375 to 0.375
- basis_grads: bfloat16 [32, 256, 256], P('blk', 'seq'), may hold values from -0.375 to 0.375
- eigenvalues: float32 [32, 256, 256], P('blk', 'seq'), may hold values from 0.05 to 5
Outputs:
- scores: float32 [8, 65536], P(None, ('seq', 'blk'))
The draws below stay inside these ranges and needn't reach their ends.
Inputs may be any that keep to these rules, and one draw needn't show every extreme that they name: `block_table`: column 0 of a row is an output-gradient block below 56, column 1 an activation block below 16; the last gradient block is named by some row. `seq_lengths`: some sequence has all 1024 tokens and some other one a quarter of them.
All inputs are finite; a program needn't handle non-finite values.
Results may differ from the reference program's by a relative error of at most 0.02.
Values may be sent and summed in bfloat16 or wider, within the bound.
A program may use at most 64 MiB of HBM per device.

```python
import math
import jax
import jax.numpy as jnp
from jax import lax

BLOCK = 256
D_WIN = 4096
FF_WIN = 14336
SEQ_LEN = 1024
QUERIES = 8
QTOK = 32
AB = 16
GB = 56
PAIRS = 32
TOKENS = 65536
SEQS = 64
QROWS = 256


def draw_block_table(key, part):
    first, second, third = jax.random.split(jax.random.fold_in(key, 11), 3)
    grad_index = jax.random.randint(first, (PAIRS,), 0, GB)
    act_index = jax.random.randint(second, (PAIRS,), 0, AB)
    chosen = jax.random.randint(third, (), 0, PAIRS)
    grad_index = jnp.where(jnp.arange(PAIRS) == chosen, GB - 1, grad_index)
    return jnp.stack([grad_index, act_index], axis=1).astype(jnp.int32)


def draw_seq_lengths(key, part):
    first, second, third = jax.random.split(jax.random.fold_in(key, 23), 3)
    lengths = jax.random.randint(first, (SEQS,), SEQ_LEN // 4, SEQ_LEN + 1)
    longest = jax.random.randint(second, (), 0, SEQS)
    shortest = (longest + 1 + jax.random.randint(third, (), 0, SEQS - 1)) % SEQS
    indices = jnp.arange(SEQS)
    lengths = jnp.where(indices == longest, SEQ_LEN, lengths)
    lengths = jnp.where(indices == shortest, SEQ_LEN // 4, lengths)
    return lengths.astype(jnp.int32)


def block_levels(own_key, shape, cuts, smallest, high):
    level = 1.0
    for dim, shards_of in cuts:
        draws = jax.random.uniform(jax.random.fold_in(jax.random.fold_in(own_key, 6), dim), (shards_of,), jnp.float32, smallest / len(cuts), high / len(cuts))
        level = level * jnp.repeat(jnp.exp(draws), shape[dim] // shards_of).reshape((-1,) + (1,) * (len(shape) - 1 - dim))
    return level


def noise(key, shape, scale, limit, cuts=(), kind=jnp.bfloat16):
    result = jax.random.normal(key, shape, jnp.float32) * scale
    if len(cuts) > 0:
        result = block_levels(key, shape, cuts, -0.22, 0.18) * result
    return jnp.clip(result, min=-limit, max=limit).astype(kind)


def setup_inputs(seed: int = 0) -> dict:
    key_of = jax.random.split(jax.random.key(seed), 10)
    return {
        "train_acts": noise(key_of[0], (TOKENS, D_WIN), 1.0, 6.0, ((0, 512),)),
        "train_grads": noise(key_of[1], (TOKENS, FF_WIN), (BLOCK * BLOCK) ** -0.5, 0.0234375, ((0, 512),)),
        "block_table": draw_block_table(jax.random.fold_in(key_of[9], 71), 0),
        "seq_lengths": draw_seq_lengths(jax.random.fold_in(key_of[9], 71), 0),
        "query_acts": noise(key_of[4], (PAIRS, QROWS, BLOCK), 1.0, 6.0, ((0, 32), (1, 16))),
        "query_grads": noise(key_of[5], (PAIRS, QROWS, BLOCK), 1.0, 6.0, ((0, 32), (1, 16))),
        "basis_acts": noise(key_of[6], (PAIRS, BLOCK, BLOCK), BLOCK ** -0.5, 0.375, ((0, 32), (1, 16))),
        "basis_grads": noise(key_of[7], (PAIRS, BLOCK, BLOCK), BLOCK ** -0.5, 0.375, ((0, 32), (1, 16))),
        "eigenvalues": jnp.clip(jnp.exp(math.log(5.0) - 4.6051702 * jax.random.uniform(key_of[8], (PAIRS, BLOCK, BLOCK), jnp.float32) ** block_levels(key_of[8], (PAIRS, BLOCK, BLOCK), ((0, 32), (1, 16)), -0.2, 0.2)), 0.05, 5.0),
    }


DAMPING = 0.1


def reference(train_acts, train_grads, block_table, seq_lengths, query_acts, query_grads, basis_acts, basis_grads, eigenvalues):
    act_blocks = train_acts.reshape(TOKENS, AB, BLOCK)
    grad_blocks = train_grads.reshape(TOKENS, GB, BLOCK)
    block_rows = math.gcd(TOKENS, 512)

    def one_pair(running, owner):
        grad_index = block_table[owner, 0]
        act_index = block_table[owner, 1]
        act_sel = jnp.take(act_blocks, act_index, axis=1)
        grad_sel = jnp.take(grad_blocks, grad_index, axis=1)
        rot_acts = jnp.dot(act_sel, basis_acts[owner], preferred_element_type=jnp.float32).astype(jnp.bfloat16)
        rot_grads = jnp.dot(grad_sel, basis_grads[owner], preferred_element_type=jnp.float32).astype(jnp.bfloat16)
        qrot_acts = jnp.dot(query_acts[owner], basis_acts[owner], preferred_element_type=jnp.float32).astype(jnp.bfloat16)
        qrot_grads = jnp.dot(query_grads[owner], basis_grads[owner], preferred_element_type=jnp.float32).astype(jnp.bfloat16)
        qrot_acts = qrot_acts.reshape(QUERIES, QTOK, BLOCK).astype(jnp.float32)
        qrot_grads = qrot_grads.reshape(QUERIES, QTOK, BLOCK).astype(jnp.float32)
        outer = jnp.einsum("qsi,qsj->qij", qrot_grads, qrot_acts)
        precond = (outer / QTOK / (eigenvalues[owner] + DAMPING)[None, :, :]).astype(jnp.bfloat16)
        right_mat = jnp.transpose(precond, (2, 0, 1)).reshape(BLOCK, QUERIES * BLOCK)

        def block_scores(pieces):
            act_piece, grad_piece = pieces
            mixed = jnp.dot(act_piece, right_mat, preferred_element_type=jnp.float32).reshape(-1, QUERIES, BLOCK)
            return jnp.sum(mixed * grad_piece.astype(jnp.float32)[:, None, :], axis=2)

        partial_value = lax.map(block_scores, (rot_acts.reshape(-1, block_rows, BLOCK), rot_grads.reshape(-1, block_rows, BLOCK)))
        return running + partial_value.reshape(TOKENS, QUERIES), None

    total, _ = lax.scan(one_pair, jnp.zeros((TOKENS, QUERIES), jnp.float32), jnp.arange(PAIRS, dtype=jnp.int32))
    position = jnp.arange(TOKENS, dtype=jnp.int32)
    valid = (position % SEQ_LEN) < seq_lengths[position // SEQ_LEN]
    return jnp.where(valid[None, :], total.T, jnp.zeros((), jnp.float32))
```

```python
import jax
import jax.numpy as jnp
from jax import lax
from jax.experimental import pallas as pl
from jax.experimental.pallas import tpu as pltpu
from jax.sharding import PartitionSpec as P

BLOCK = 256
SEQ_LEN = 1024
QUERIES = 8
QTOK = 32
DAMPING = 0.1
MESH = pl.DeviceIdType.MESH

NX, NY, NC = 4, 4, 2
CHIPS = NX * NY
NB = CHIPS * NC
NZ = 16
SHARD = 16
TOK = 128

HOPS = (0, 1, 2, 1)
FAR_FIRST = sorted(
    [(dy, dx) for dy in range(NY) for dx in range(NX)],
    key=lambda o: -(HOPS[o[0]] + HOPS[o[1]]),
)
WORK_ORDER = [(0, 0)] + FAR_FIRST[:-1]


def pick(step, values):
    result = 0
    for place, value in enumerate(values):
        result = result + jnp.where(step == place, value, 0)
    return result


def kernel(
    acts_hbm, grads_hbm, table, qa_ref, qg_ref, ba_ref, bg_ref, eig_ref,
    out_ref,
    acts, grads, send, recv, weights, act_t, grad_t, right, ret_send, ret_recv,
    load_sem, send_sem, recv_sem, up_sem, down_sem, ring_sem, back_sem, home_sem,
):
    z = lax.axis_index("seq")
    b = lax.axis_index("blk")
    chip = b // NC
    core = b % NC
    y, x = chip // NX, chip % NX
    above, below = (z + 1) % NZ, (z + NZ - 1) % NZ

    for hbm, blocks, sem in ((acts_hbm, acts, 0), (grads_hbm, grads, 1)):

        @pl.loop(0, blocks.shape[0])
        def _(block):
            columns = pl.ds(pl.multiple_of(block * BLOCK, BLOCK), BLOCK)
            pltpu.make_async_copy(hbm.at[:, columns], blocks.at[block], load_sem.at[sem]).start()

    barrier = pltpu.get_barrier_semaphore()

    @pl.loop(1, NB)
    def _(step):
        pl.semaphore_signal(barrier, inc=1, device_id=(z, (b + step) % NB), device_id_type=MESH)

    pl.semaphore_signal(barrier, inc=1, device_id=(above, b), device_id_type=MESH)
    pl.semaphore_signal(barrier, inc=1, device_id=(below, b), device_id_type=MESH)

    weights[z, 0:16] = ba_ref[0]
    weights[z, 16:32] = bg_ref[0]
    weights[z, 32:48] = qa_ref[0]
    weights[z, 48:64] = qg_ref[0]
    weights[z, 64:80] = (eig_ref[0] + DAMPING).astype(jnp.bfloat16)

    pl.semaphore_wait(barrier, NB + 1)

    def ring_up(step):
        slot = (z + NZ - step) % NZ
        return pltpu.make_async_remote_copy(
            weights.at[slot], weights.at[slot], up_sem.at[step], ring_sem.at[slot],
            device_id=(above, b), device_id_type=MESH)

    def ring_down(step):
        slot = (z + step) % NZ
        return pltpu.make_async_remote_copy(
            weights.at[slot], weights.at[slot], down_sem.at[step], ring_sem.at[slot],
            device_id=(below, b), device_id_type=MESH)

    ring_up(0).start()
    ring_down(0).start()
    for blocks, sem in ((acts, 0), (grads, 1)):
        pltpu.make_async_copy(blocks, blocks, load_sem.at[sem]).wait()

    def token_copy(peer):
        return pltpu.make_async_remote_copy(
            send.at[peer], recv.at[b], send_sem.at[peer], recv_sem.at[b],
            device_id=(z, peer), device_id_type=MESH)

    def select(owner):
        return acts[table[owner, 1]], grads[table[owner, 0]]

    @pl.loop(0, CHIPS)
    def _(step):
        offset = pick(step, [dy * NX + dx for dy, dx in FAR_FIRST])
        to_chip = ((y + offset // NX) % NY) * NX + (x + offset % NX) % NX
        for c in range(NC):
            peer = to_chip * NC + c
            act_sel, grad_sel = select(peer)

            @pl.when(peer != b)
            def _():
                send[peer, :, 0:BLOCK] = act_sel
                send[peer, :, BLOCK : 2 * BLOCK] = grad_sel
                token_copy(peer).start()

            @pl.when(peer == b)
            def _():
                recv[peer, :, 0:BLOCK] = act_sel
                recv[peer, :, BLOCK : 2 * BLOCK] = grad_sel

    def arrived(slot):
        pltpu.make_async_remote_copy(
            weights.at[slot], weights.at[slot], up_sem.at[0], ring_sem.at[slot],
            device_id=(above, b), device_id_type=MESH).wait_recv()

    @pl.loop(1, NZ // 2)
    def _(step):
        arrived((z + NZ - step) % NZ)
        ring_up(step).start()
        arrived((z + step) % NZ)

        @pl.when(step < NZ // 2 - 1)
        def _():
            ring_down(step).start()

    arrived((z + NZ // 2) % NZ)

    def gathered(place):
        return weights[:, place * SHARD : (place + 1) * SHARD, :].reshape(BLOCK, BLOCK)

    def dot(lhs, rhs, dims):
        return lax.dot_general(lhs, rhs, (dims, ((), ())), preferred_element_type=jnp.float32)

    basis_act, basis_grad = gathered(0), gathered(1)
    act_t[...] = basis_act.astype(jnp.float32).T.astype(jnp.bfloat16)
    grad_t[...] = basis_grad.astype(jnp.float32).T.astype(jnp.bfloat16)
    qrot_acts = dot(gathered(2), basis_act, ((1,), (0,))).astype(jnp.bfloat16)
    qrot_grads = dot(gathered(3), basis_grad, ((1,), (0,))).astype(jnp.bfloat16)
    scale = 1.0 / (gathered(4).astype(jnp.float32) * QTOK)
    for q in range(QUERIES):
        rows = slice(q * QTOK, (q + 1) * QTOK)
        outer = dot(qrot_grads[rows], qrot_acts[rows], ((0,), (0,)))
        right[q * BLOCK : (q + 1) * BLOCK, :] = (outer * scale).astype(jnp.bfloat16)

    def return_copy(peer):
        return pltpu.make_async_remote_copy(
            ret_send.at[peer], ret_recv.at[b], back_sem.at[peer], home_sem.at[b],
            device_id=(z, peer), device_id_type=MESH)

    @pl.loop(0, CHIPS)
    def _(step):
        offset = pick(step, [dy * NX + dx for dy, dx in WORK_ORDER])
        from_chip = ((y + NY - offset // NX) % NY) * NX + (x + NX - offset % NX) % NX
        for c in range(NC):
            peer = from_chip * NC + c

            @pl.when(peer != b)
            def _():
                pltpu.make_async_remote_copy(
                    send.at[peer], recv.at[peer], send_sem.at[peer], recv_sem.at[peer],
                    device_id=(z, peer), device_id_type=MESH).wait_recv()

        tokens = recv[pl.ds(from_chip * NC, NC)].reshape(NC * TOK, 2 * BLOCK)
        rot_acts = dot(act_t[...], tokens[:, 0:BLOCK], ((1,), (1,))).astype(jnp.bfloat16)
        rot_grads = dot(grad_t[...], tokens[:, BLOCK:], ((1,), (1,))).astype(jnp.bfloat16)
        rot_grads = rot_grads.astype(jnp.float32)
        for q in range(QUERIES):
            mixed = dot(right[q * BLOCK : (q + 1) * BLOCK, :], rot_acts, ((1,), (0,)))
            score = jnp.sum(mixed * rot_grads, axis=0, keepdims=True)
            for c in range(NC):
                ret_send[from_chip * NC + c, q : q + 1, :] = score[:, c * TOK : (c + 1) * TOK]
        for c in range(NC):
            peer = from_chip * NC + c

            @pl.when(peer != b)
            def _():
                return_copy(peer).start()

    ret_recv[b] = ret_send[b]

    @pl.loop(1, NB)
    def _(step):
        peer = (b + step) % NB
        pltpu.make_async_remote_copy(
            ret_send.at[peer], ret_recv.at[peer], back_sem.at[peer], home_sem.at[peer],
            device_id=(z, peer), device_id_type=MESH).wait_recv()

    total = ret_recv[0]
    for source in range(1, NB):
        total = total + ret_recv[source]
    out_ref[...] = total

    @pl.loop(1, NB)
    def _(step):
        peer = (b + step) % NB
        token_copy(peer).wait_send()
        return_copy(peer).wait_send()

    @pl.loop(0, NZ // 2)
    def _(step):
        ring_up(step).wait_send()

    @pl.loop(0, NZ // 2 - 1)
    def _(step):
        ring_down(step).wait_send()


def on_device(
    train_acts, train_grads, block_table, seq_lengths,
    query_acts, query_grads, basis_acts, basis_grads, eigenvalues,
):
    bf16, f32 = jnp.bfloat16, jnp.float32
    vmem = pl.BlockSpec(memory_space=pltpu.VMEM)
    smem = pl.BlockSpec(memory_space=pltpu.SMEM)
    hbm = pl.BlockSpec(memory_space=pl.ANY)
    dma = pltpu.SemaphoreType.DMA
    scores = pl.pallas_call(
        kernel,
        out_shape=jax.ShapeDtypeStruct((QUERIES, TOK), f32),
        in_specs=[hbm, hbm, smem] + [vmem] * 5,
        out_specs=vmem,
        scratch_shapes=[
            pltpu.VMEM((train_acts.shape[1] // BLOCK, TOK, BLOCK), bf16),
            pltpu.VMEM((train_grads.shape[1] // BLOCK, TOK, BLOCK), bf16),
            pltpu.VMEM((NB, TOK, 2 * BLOCK), bf16),
            pltpu.VMEM((NB, TOK, 2 * BLOCK), bf16),
            pltpu.VMEM((NZ, 5 * SHARD, BLOCK), bf16),
            pltpu.VMEM((BLOCK, BLOCK), bf16),
            pltpu.VMEM((BLOCK, BLOCK), bf16),
            pltpu.VMEM((QUERIES * BLOCK, BLOCK), bf16),
            pltpu.VMEM((NB, QUERIES, TOK), f32),
            pltpu.VMEM((NB, QUERIES, TOK), f32),
            dma((2,)), dma((NB,)), dma((NB,)), dma((NZ // 2,)), dma((NZ // 2,)),
            dma((NZ,)), dma((NB,)), dma((NB,)),
        ],
        compiler_params=pltpu.CompilerParams(
            collective_id=0, has_side_effects=True, vmem_limit_bytes=48 * 2**20),
    )(train_acts, train_grads, block_table,
      query_acts, query_grads, basis_acts, basis_grads, eigenvalues)
    base = (lax.axis_index("seq") * NB + lax.axis_index("blk")) * TOK
    place = base % SEQ_LEN + lax.broadcasted_iota(jnp.int32, (QUERIES, TOK), 1)
    return jnp.where(place < seq_lengths[base // SEQ_LEN], scores, 0.0)


def solution(mesh):
    in_specs = (
        P(("seq", "blk"), None),
        P(("seq", "blk"), None),
        P(),
        P(),
        P("blk", "seq", None),
        P("blk", "seq", None),
        P("blk", "seq", None),
        P("blk", "seq", None),
        P("blk", "seq", None),
    )
    return jax.shard_map(
        on_device, mesh=mesh, in_specs=in_specs, out_specs=P(None, ("seq", "blk")),
        check_vma=False)
```

```python
import jax
import jax.numpy as jnp
from jax import lax
from jax.experimental import pallas as pl
from jax.experimental.pallas import tpu as pltpu
from jax.sharding import PartitionSpec as P

BLOCK = 256
SEQ_LEN = 1024
QUERIES = 8
QTOK = 32
DAMPING = 0.1
MESH = pl.DeviceIdType.MESH

SIDE = 4
NC = 2
NB = SIDE * SIDE * NC
NZ = 16
SHARD = 16
TOK = 128


def wrap(i, n=SIDE):
    return lax.rem(i + n, n)


def blk_of(y, x, core):
    return (wrap(y) * SIDE + wrap(x)) * NC + core


def dot(lhs, rhs, dims):
    return lax.dot_general(lhs, rhs, (dims, ((), ())), preferred_element_type=jnp.float32)


def kernel(
    acts_hbm, grads_hbm, qa_hbm, qg_hbm, ba_hbm, bg_hbm, eig_hbm, table, lengths,
    out_ref,
    acts, grads, eig, send, recv, weights, act_t, grad_t, right, scores, home,
    load_sem, shard_sem, send_sem, recv_sem, up_sem, down_sem, ring_sem,
    spread_sem, held_sem, back_sem, home_sem,
):
    z = lax.axis_index("seq")
    b = lax.axis_index("blk")
    core = lax.rem(b, NC)
    chip = lax.div(b, NC)
    y, x = lax.div(chip, SIDE), lax.rem(chip, SIDE)
    above, below = wrap(z + 1, NZ), wrap(z - 1, NZ)

    def holder(kind, j):
        return (z, blk_of(y + j, x, 0) if kind == 0 else blk_of(y, x + j, 1))

    def pair(kind, j, h):
        return blk_of(y + j, x + h, 0) if kind == 0 else blk_of(y + h, x + j, 1)

    def source(j, c):
        return (z, jnp.where(core == 0, blk_of(y - j, x, c), blk_of(y, x - j, c)))

    def fellow(h):
        return (z, jnp.where(core == 0, blk_of(y, x - h, 0), blk_of(y - h, x, 1)))

    shards = [
        pltpu.make_async_copy(
            hbm.at[0], weights.at[0, z, pl.ds(place * SHARD, SHARD)], shard_sem.at[place])
        for place, hbm in enumerate((ba_hbm, bg_hbm, qa_hbm, qg_hbm))
    ] + [pltpu.make_async_copy(eig_hbm.at[0], eig, shard_sem.at[4])]
    for copy in shards:
        copy.start()
    for hbm, blocks, sem in ((acts_hbm, acts, 0), (grads_hbm, grads, 1)):

        @pl.loop(0, blocks.shape[0])
        def _(block):
            columns = pl.ds(pl.multiple_of(block * BLOCK, BLOCK), BLOCK)
            pltpu.make_async_copy(hbm.at[:, columns], blocks.at[block], load_sem.at[sem]).start()

    barrier = pltpu.get_barrier_semaphore()
    greeted = [(z, blk_of(y, x, 1 - core)), (above, b), (below, b)]
    for j in range(1, SIDE):
        for c in range(NC):
            greeted += [(z, blk_of(y + j, x, c)), (z, blk_of(y, x + j, c))]
    for peer in greeted:
        pl.semaphore_signal(barrier, inc=1, device_id=peer, device_id_type=MESH)

    for copy in shards:
        copy.wait()
    weights[0, z, 4 * SHARD : 5 * SHARD] = (eig[...] + DAMPING).astype(jnp.bfloat16)
    pl.semaphore_wait(barrier, len(greeted))

    def ring(step, direction):
        slot, to, sems = (
            (wrap(z - step, NZ), above, up_sem) if direction > 0
            else (wrap(z + step, NZ), below, down_sem))
        piece = weights.at[0, slot]
        return pltpu.make_async_remote_copy(
            piece, piece, sems.at[step], ring_sem.at[slot],
            device_id=(to, b), device_id_type=MESH)

    def arrived(slot):
        piece = weights.at[0, slot]
        pltpu.make_async_remote_copy(
            piece, piece, up_sem.at[0], ring_sem.at[slot],
            device_id=(above, b), device_id_type=MESH).wait_recv()

    def spread(slot):
        for h in range(1, SIDE):
            pltpu.make_async_remote_copy(
                weights.at[0, slot], weights.at[h, slot], spread_sem.at[h], held_sem.at[h],
                device_id=fellow(h), device_id_type=MESH).start()

    def token_copy(kind, j, h):
        return pltpu.make_async_remote_copy(
            send.at[h, kind, j], recv.at[h, j, core], send_sem.at[h, kind, j],
            recv_sem.at[h, j, core], device_id=holder(kind, j), device_id_type=MESH)

    def dispatch(h):
        for j in (0, 2, 1, 3):
            for kind in range(NC):
                owner = pair(kind, j, h)
                act_sel, grad_sel = acts[table[1, owner]], grads[table[0, owner]]

                def to_peer():
                    send[h, kind, j, :, 0:BLOCK] = act_sel
                    send[h, kind, j, :, BLOCK : 2 * BLOCK] = grad_sel
                    token_copy(kind, j, h).start()

                def to_self():
                    recv[h, 0, core, :, 0:BLOCK] = act_sel
                    recv[h, 0, core, :, BLOCK : 2 * BLOCK] = grad_sel

                if j == 0:
                    pl.when(core != kind)(to_peer)
                    pl.when(core == kind)(to_self)
                else:
                    to_peer()

    ring(0, 1).start()
    ring(0, -1).start()
    spread(z)
    for blocks, sem in ((acts, 0), (grads, 1)):
        pltpu.make_async_copy(blocks, blocks, load_sem.at[sem]).wait()

    @pl.loop(1, NZ // 2)
    def _(step):
        @pl.when(step <= SIDE)
        def _():
            dispatch(step - 1)

        arrived(wrap(z - step, NZ))
        ring(step, 1).start()
        arrived(wrap(z + step, NZ))

        @pl.when(step < NZ // 2 - 1)
        def _():
            ring(step, -1).start()

        spread(wrap(z - step, NZ))
        spread(wrap(z + step, NZ))

    arrived(wrap(z + NZ // 2, NZ))
    spread(wrap(z + NZ // 2, NZ))

    def prepare(h):
        def gathered(place):
            rows = weights[h, :, place * SHARD : (place + 1) * SHARD, :]
            return rows.reshape(BLOCK, BLOCK)

        basis_act, basis_grad = gathered(0), gathered(1)
        act_t[...] = basis_act.astype(jnp.float32).T.astype(jnp.bfloat16)
        grad_t[...] = basis_grad.astype(jnp.float32).T.astype(jnp.bfloat16)
        qrot_acts = dot(gathered(2), basis_act, ((1,), (0,))).astype(jnp.bfloat16)
        qrot_grads = dot(gathered(3), basis_grad, ((1,), (0,))).astype(jnp.bfloat16)
        scale = 1.0 / (gathered(4).astype(jnp.float32) * QTOK)
        for q in range(QUERIES):
            rows = slice(q * QTOK, (q + 1) * QTOK)
            outer = dot(qrot_grads[rows], qrot_acts[rows], ((0,), (0,)))
            right[q * BLOCK : (q + 1) * BLOCK, :] = (outer * scale).astype(jnp.bfloat16)

    def return_copy(j, c):
        return pltpu.make_async_remote_copy(
            scores.at[j, c], home.at[core, j], back_sem.at[j, c], home_sem.at[core, j],
            device_id=source(j, c), device_id_type=MESH)

    def is_self(j, c):
        return jnp.logical_and(j == 0, c == core)

    @pl.loop(0, SIDE)
    def _(h):
        @pl.when(h > 0)
        def _():
            pltpu.make_async_remote_copy(
                weights.at[0], weights.at[h], spread_sem.at[h], held_sem.at[h],
                device_id=fellow(h), device_id_type=MESH).wait_recv()

        prepare(h)

        @pl.loop(0, SIDE)
        def _(j):
            for c in range(NC):

                @pl.when(jnp.logical_not(is_self(j, c)))
                def _():
                    pltpu.make_async_remote_copy(
                        send.at[h, 0, j], recv.at[h, j, c], send_sem.at[h, 0, j],
                        recv_sem.at[h, j, c], device_id=source(j, c),
                        device_id_type=MESH).wait_recv()

            tokens = recv[h, j].reshape(NC * TOK, 2 * BLOCK)
            rot_acts = dot(act_t[...], tokens[:, 0:BLOCK], ((1,), (1,))).astype(jnp.bfloat16)
            rot_grads = dot(grad_t[...], tokens[:, BLOCK:], ((1,), (1,))).astype(jnp.bfloat16)
            rot_grads = rot_grads.astype(jnp.float32)
            parts = []
            for q in range(QUERIES):
                mixed = dot(right[q * BLOCK : (q + 1) * BLOCK, :], rot_acts, ((1,), (0,)))
                parts.append(jnp.sum(mixed * rot_grads, axis=0, keepdims=True))
            score = jnp.concatenate(parts, axis=0)
            for c in range(NC):
                part = score[:, c * TOK : (c + 1) * TOK]

                @pl.when(h == 0)
                def _():
                    scores[j, c] = part

                @pl.when(h > 0)
                def _():
                    scores[j, c] = scores[j, c] + part

                @pl.when(jnp.logical_and(h == SIDE - 1, jnp.logical_not(is_self(j, c))))
                def _():
                    return_copy(j, c).start()

    home[core, 0] = scores[0, core]
    for kind in range(NC):
        for j in range(SIDE):

            def wait_home():
                pltpu.make_async_remote_copy(
                    scores.at[j, 0], home.at[kind, j], back_sem.at[j, 0], home_sem.at[kind, j],
                    device_id=holder(kind, j), device_id_type=MESH).wait_recv()

            if j == 0:
                pl.when(core != kind)(wait_home)
            else:
                wait_home()

    total = home[0, 0]
    for kind in range(NC):
        for j in range(SIDE):
            if kind + j > 0:
                total = total + home[kind, j]
    base = (z * NB + b) * TOK
    place = lax.rem(base, SEQ_LEN) + lax.broadcasted_iota(jnp.int32, (QUERIES, TOK), 1)
    out_ref[...] = jnp.where(place < lengths[lax.div(base, SEQ_LEN)], total, 0.0)

    for j in range(SIDE):
        for kind in range(NC):

            def wait_sent():
                @pl.loop(0, SIDE)
                def _(h):
                    token_copy(kind, j, h).wait_send()

                return_copy(j, kind).wait_send()

            if j == 0:
                pl.when(core != kind)(wait_sent)
            else:
                wait_sent()

    @pl.loop(0, NZ // 2)
    def _(step):
        ring(step, 1).wait_send()

    @pl.loop(0, NZ // 2 - 1)
    def _(step):
        ring(step, -1).wait_send()

    for h in range(1, SIDE):
        pltpu.make_async_remote_copy(
            weights.at[0], weights.at[h], spread_sem.at[h], held_sem.at[h],
            device_id=fellow(h), device_id_type=MESH).wait_send()


def on_device(
    train_acts, train_grads, block_table, seq_lengths,
    query_acts, query_grads, basis_acts, basis_grads, eigenvalues,
):
    bf16, f32 = jnp.bfloat16, jnp.float32
    vmem = pl.BlockSpec(memory_space=pltpu.VMEM)
    smem = pl.BlockSpec(memory_space=pltpu.SMEM)
    hbm = pl.BlockSpec(memory_space=pltpu.HBM)
    dma = pltpu.SemaphoreType.DMA
    return pl.pallas_call(
        kernel,
        out_shape=jax.ShapeDtypeStruct((QUERIES, TOK), f32),
        in_specs=[hbm] * 7 + [smem, smem],
        out_specs=vmem,
        scratch_shapes=[
            pltpu.VMEM((train_acts.shape[1] // BLOCK, TOK, BLOCK), bf16),
            pltpu.VMEM((train_grads.shape[1] // BLOCK, TOK, BLOCK), bf16),
            pltpu.VMEM((SHARD, BLOCK), f32),
            pltpu.VMEM((SIDE, NC, SIDE, TOK, 2 * BLOCK), bf16),
            pltpu.VMEM((SIDE, SIDE, NC, TOK, 2 * BLOCK), bf16),
            pltpu.VMEM((SIDE, NZ, 5 * SHARD, BLOCK), bf16),
            pltpu.VMEM((BLOCK, BLOCK), bf16),
            pltpu.VMEM((BLOCK, BLOCK), bf16),
            pltpu.VMEM((QUERIES * BLOCK, BLOCK), bf16),
            pltpu.VMEM((SIDE, NC, QUERIES, TOK), f32),
            pltpu.VMEM((NC, SIDE, QUERIES, TOK), f32),
            dma((2,)), dma((5,)), dma((SIDE, NC, SIDE)), dma((SIDE, SIDE, NC)),
            dma((NZ // 2,)), dma((NZ // 2,)), dma((NZ,)),
            dma((SIDE,)), dma((SIDE,)), dma((SIDE, NC)), dma((NC, SIDE)),
        ],
        compiler_params=pltpu.CompilerParams(
            collective_id=0, has_side_effects=True, vmem_limit_bytes=48 * 2**20),
    )(train_acts, train_grads, query_acts, query_grads, basis_acts, basis_grads, eigenvalues,
      block_table.T, seq_lengths)


def solution(mesh):
    in_specs = (
        P(("seq", "blk"), None),
        P(("seq", "blk"), None),
        P(),
        P(),
        P("blk", "seq", None),
        P("blk", "seq", None),
        P("blk", "seq", None),
        P("blk", "seq", None),
        P("blk", "seq", None),
    )
    return jax.shard_map(
        on_device, mesh=mesh, in_specs=in_specs, out_specs=P(None, ("seq", "blk")),
        check_vma=False)
```

```python
import jax
import jax.numpy as jnp
from jax import lax
from jax.experimental import pallas as pl
from jax.experimental.pallas import tpu as pltpu
from jax.sharding import PartitionSpec as P

BLOCK = 256
SEQ_LEN = 1024
QUERIES = 8
QTOK = 32
DAMPING = 0.1
MESH = pl.DeviceIdType.MESH

SIDE = 4
NC = 2
NB = SIDE * SIDE * NC
NZ = 16
SHARD = 16
TOK = 128


def wrap(i, n=SIDE):
    return lax.rem(i + n, n)


def blk_of(y, x, core):
    return (wrap(y) * SIDE + wrap(x)) * NC + core


def dot(lhs, rhs, dims):
    return lax.dot_general(lhs, rhs, (dims, ((), ())), preferred_element_type=jnp.float32)


def kernel(
    acts_hbm, grads_hbm, qa_hbm, qg_hbm, ba_hbm, bg_hbm, eig_hbm, table, lengths,
    out_ref,
    acts, grads, eig, raw, send, recv, weights, act_t, grad_t, right, scores, home,
    load_sem, shard_sem, send_sem, recv_sem, up_sem, swap_sem, ring_sem,
    spread_sem, held_sem, back_sem, home_sem,
):
    z = lax.axis_index("seq")
    b = lax.axis_index("blk")
    core = lax.rem(b, NC)
    chip = lax.div(b, NC)
    y, x = lax.div(chip, SIDE), lax.rem(chip, SIDE)

    twist = 2 * lax.rem(z, 2)

    def holder(kind, j):
        if j == 2:
            return (wrap(z + (1 if kind == 0 else NZ - 1), NZ), blk_of(y, x, kind))
        return (z, blk_of(y + j, x, 0) if kind == 0 else blk_of(y, x + j, 1))

    def pair(kind, j, h):
        if kind == 0:
            return blk_of(wrap(y + j + twist), x + h, 0)
        return blk_of(y + h, wrap(x + j + twist), 1)

    def source(j, c):
        far = j == 2
        plane = jnp.where(far, wrap(z + jnp.where(core == 0, NZ - 1, 1), NZ), z)
        step = jnp.where(far, 0, SIDE - j)
        return (plane, jnp.where(core == 0, blk_of(y + step, x, c), blk_of(y, x + step, c)))

    def fellow(h):
        return (z, jnp.where(core == 0, blk_of(y, x - h, 0), blk_of(y - h, x, 1)))

    def beside():
        return jnp.where(core == 0, blk_of(y + 2, x, 0), blk_of(y, x + 2, 1))

    def column(to):
        return (wrap(z + to, NZ), beside() if to % 2 else b)

    shards = [
        pltpu.make_async_copy(
            hbm.at[0], raw.at[pl.ds(place * SHARD, SHARD)], shard_sem.at[place])
        for place, hbm in enumerate((ba_hbm, bg_hbm, qa_hbm, qg_hbm))
    ] + [pltpu.make_async_copy(eig_hbm.at[0], eig, shard_sem.at[4])]
    for copy in shards:
        copy.start()
    for hbm, blocks, sem in ((acts_hbm, acts, 0), (grads_hbm, grads, 1)):

        @pl.loop(0, blocks.shape[0])
        def _(block):
            columns = pl.ds(pl.multiple_of(block * BLOCK, BLOCK), BLOCK)
            pltpu.make_async_copy(hbm.at[:, columns], blocks.at[block], load_sem.at[sem]).start()

    barrier = pltpu.get_barrier_semaphore()
    greeted = [(z, blk_of(y, x, 1 - core))]
    for j in range(1, SIDE):
        for c in range(NC):
            greeted += [(z, blk_of(y + j, x, c)), (z, blk_of(y, x + j, c))]
    for step in (2, 4, 8, NZ - 4, NZ - 2):
        greeted.append((wrap(z + step, NZ), b))
    for step in (1, NZ - 1):
        greeted.append((wrap(z + step, NZ), beside()))
        for c in range(NC):
            greeted.append((wrap(z + step, NZ), blk_of(y, x, c)))
    for peer in greeted:
        pl.semaphore_signal(barrier, inc=1, device_id=peer, device_id_type=MESH)

    for copy in shards:
        copy.wait()
    raw[4 * SHARD : 5 * SHARD] = (eig[...] + DAMPING).astype(jnp.bfloat16)
    pl.semaphore_wait(barrier, len(greeted))

    def piece_copy(slot, to):
        piece = weights.at[0, slot]
        return pltpu.make_async_remote_copy(
            piece, piece, up_sem.at[0], ring_sem.at[slot],
            device_id=column(to), device_id_type=MESH)

    def arrived(step):
        slot = wrap(z + step, NZ)
        piece_copy(slot, 1).wait_recv()
        return slot

    def spread_copy(piece, h):
        return pltpu.make_async_remote_copy(
            weights.at[0, piece], weights.at[h, piece], spread_sem.at[h], held_sem.at[h],
            device_id=fellow(h), device_id_type=MESH)

    def spread(slot):
        for h in (1, 3):
            spread_copy(slot, h).start()

    swap = pltpu.make_async_remote_copy(
        raw, weights.at[0, z], swap_sem.at[0], ring_sem.at[z],
        device_id=(z, beside()), device_id_type=MESH)

    def token_copy(kind, j, h):
        return pltpu.make_async_remote_copy(
            send.at[h, kind, j], recv.at[h, j, core], send_sem.at[h, kind, j],
            recv_sem.at[h, j, core], device_id=holder(kind, j), device_id_type=MESH)

    def dispatch(h, offsets):
        for j in offsets:
            for kind in range(NC):
                owner = pair(kind, j, h)
                act_sel, grad_sel = acts[table[1, owner]], grads[table[0, owner]]

                def to_peer():
                    send[h, kind, j, :, 0:BLOCK] = act_sel
                    send[h, kind, j, :, BLOCK : 2 * BLOCK] = grad_sel
                    token_copy(kind, j, h).start()

                def to_self():
                    recv[h, 0, core, :, 0:BLOCK] = act_sel
                    recv[h, 0, core, :, BLOCK : 2 * BLOCK] = grad_sel

                if j == 0:
                    pl.when(core != kind)(to_peer)
                    pl.when(core == kind)(to_self)
                else:
                    to_peer()

    def hand_on(slot, steps):
        for to in steps:
            piece_copy(slot, to).start()
        spread(slot)

    @pl.when(twist > 0)
    def _():
        swap.start()
        swap.wait()

    @pl.when(twist == 0)
    def _():
        weights[0, z] = raw[...]

    hand_on(z, (4, NZ - 4, 8, 1, NZ - 1, 2, NZ - 2))
    for blocks, sem in ((acts, 0), (grads, 1)):
        pltpu.make_async_copy(blocks, blocks, load_sem.at[sem]).wait()
    dispatch(0, (0, 1, 3))
    dispatch(1, (0, 1, 3))
    for step in (4, NZ - 4):
        hand_on(arrived(step), (1, NZ - 1))
    hand_on(arrived(8), (1, NZ - 1, 2, NZ - 2))
    dispatch(0, (2,))
    dispatch(1, (2,))
    dispatch(3, (0, 1, 3))
    for step in (1, NZ - 1, 2, NZ - 2):
        spread(arrived(step))
    dispatch(3, (2,))
    dispatch(2, (0, 1, 3, 2))
    for step in (5, 13, 3, 11, 9, 7, 10, 6):
        spread(arrived(step))
    every = pl.ds(0, NZ)
    spread_copy(every, 2).start()

    def prepare(h):
        def gathered(place):
            rows = weights[h, :, place * SHARD : (place + 1) * SHARD, :]
            return rows.reshape(BLOCK, BLOCK)

        basis_act, basis_grad = gathered(0), gathered(1)
        act_t[...] = basis_act.astype(jnp.float32).T.astype(jnp.bfloat16)
        grad_t[...] = basis_grad.astype(jnp.float32).T.astype(jnp.bfloat16)
        qrot_acts = dot(gathered(2), basis_act, ((1,), (0,))).astype(jnp.bfloat16)
        qrot_grads = dot(gathered(3), basis_grad, ((1,), (0,))).astype(jnp.bfloat16)
        scale = 1.0 / (gathered(4).astype(jnp.float32) * QTOK)
        for q in range(QUERIES):
            rows = slice(q * QTOK, (q + 1) * QTOK)
            outer = dot(qrot_grads[rows], qrot_acts[rows], ((0,), (0,)))
            right[q * BLOCK : (q + 1) * BLOCK, :] = (outer * scale).astype(jnp.bfloat16)

    def return_copy(j, c):
        return pltpu.make_async_remote_copy(
            scores.at[j, c], home.at[core, j], back_sem.at[j, c], home_sem.at[core, j],
            device_id=source(j, c), device_id_type=MESH)

    def is_self(j, c):
        return jnp.logical_and(j == 0, c == core)

    @pl.loop(0, SIDE)
    def _(turn):
        h = lax.rem(turn * (turn + 1) // 2, SIDE)

        @pl.when(h > 0)
        def _():
            spread_copy(every, h).wait_recv()

        prepare(h)

        @pl.loop(0, SIDE)
        def _(j):
            for c in range(NC):

                @pl.when(jnp.logical_not(is_self(j, c)))
                def _():
                    pltpu.make_async_remote_copy(
                        send.at[h, 0, j], recv.at[h, j, c], send_sem.at[h, 0, j],
                        recv_sem.at[h, j, c], device_id=source(j, c),
                        device_id_type=MESH).wait_recv()

            tokens = recv[h, j].reshape(NC * TOK, 2 * BLOCK)
            rot_acts = dot(act_t[...], tokens[:, 0:BLOCK], ((1,), (1,))).astype(jnp.bfloat16)
            rot_grads = dot(grad_t[...], tokens[:, BLOCK:], ((1,), (1,))).astype(jnp.bfloat16)
            rot_grads = rot_grads.astype(jnp.float32)
            parts = []
            for q in range(QUERIES):
                mixed = dot(right[q * BLOCK : (q + 1) * BLOCK, :], rot_acts, ((1,), (0,)))
                parts.append(jnp.sum(mixed * rot_grads, axis=0, keepdims=True))
            score = jnp.concatenate(parts, axis=0)
            for c in range(NC):
                part = score[:, c * TOK : (c + 1) * TOK]

                @pl.when(turn == 0)
                def _():
                    scores[j, c] = part

                @pl.when(turn > 0)
                def _():
                    scores[j, c] = scores[j, c] + part

                @pl.when(jnp.logical_and(turn == SIDE - 1, jnp.logical_not(is_self(j, c))))
                def _():
                    return_copy(j, c).start()

    home[core, 0] = scores[0, core]
    for kind in range(NC):
        for j in range(SIDE):

            def wait_home():
                pltpu.make_async_remote_copy(
                    scores.at[j, 0], home.at[kind, j], back_sem.at[j, 0], home_sem.at[kind, j],
                    device_id=holder(kind, j), device_id_type=MESH).wait_recv()

            if j == 0:
                pl.when(core != kind)(wait_home)
            else:
                wait_home()

    total = home[0, 0]
    for kind in range(NC):
        for j in range(SIDE):
            if kind + j > 0:
                total = total + home[kind, j]
    base = (z * NB + b) * TOK
    place = lax.rem(base, SEQ_LEN) + lax.broadcasted_iota(jnp.int32, (QUERIES, TOK), 1)
    out_ref[...] = jnp.where(place < lengths[lax.div(base, SEQ_LEN)], total, 0.0)

    for j in range(SIDE):
        for kind in range(NC):

            def wait_sent():
                @pl.loop(0, SIDE)
                def _(h):
                    token_copy(kind, j, h).wait_send()

                return_copy(j, kind).wait_send()

            if j == 0:
                pl.when(core != kind)(wait_sent)
            else:
                wait_sent()

    gone = weights.at[0, pl.ds(0, NZ - 1)]
    pltpu.make_async_remote_copy(
        gone, gone, up_sem.at[0], ring_sem.at[0], device_id=(wrap(z + 1, NZ), b),
        device_id_type=MESH).wait_send()
    for h in range(1, SIDE):
        spread_copy(every, h).wait_send()


def on_device(
    train_acts, train_grads, block_table, seq_lengths,
    query_acts, query_grads, basis_acts, basis_grads, eigenvalues,
):
    bf16, f32 = jnp.bfloat16, jnp.float32
    vmem = pl.BlockSpec(memory_space=pltpu.VMEM)
    smem = pl.BlockSpec(memory_space=pltpu.SMEM)
    hbm = pl.BlockSpec(memory_space=pltpu.HBM)
    dma = pltpu.SemaphoreType.DMA
    return pl.pallas_call(
        kernel,
        out_shape=jax.ShapeDtypeStruct((QUERIES, TOK), f32),
        in_specs=[hbm] * 7 + [smem, smem],
        out_specs=vmem,
        scratch_shapes=[
            pltpu.VMEM((train_acts.shape[1] // BLOCK, TOK, BLOCK), bf16),
            pltpu.VMEM((train_grads.shape[1] // BLOCK, TOK, BLOCK), bf16),
            pltpu.VMEM((SHARD, BLOCK), f32),
            pltpu.VMEM((5 * SHARD, BLOCK), bf16),
            pltpu.VMEM((SIDE, NC, SIDE, TOK, 2 * BLOCK), bf16),
            pltpu.VMEM((SIDE, SIDE, NC, TOK, 2 * BLOCK), bf16),
            pltpu.VMEM((SIDE, NZ, 5 * SHARD, BLOCK), bf16),
            pltpu.VMEM((BLOCK, BLOCK), bf16),
            pltpu.VMEM((BLOCK, BLOCK), bf16),
            pltpu.VMEM((QUERIES * BLOCK, BLOCK), bf16),
            pltpu.VMEM((SIDE, NC, QUERIES, TOK), f32),
            pltpu.VMEM((NC, SIDE, QUERIES, TOK), f32),
            dma((2,)), dma((5,)), dma((SIDE, NC, SIDE)), dma((SIDE, SIDE, NC)),
            dma((1,)), dma((1,)), dma((NZ,)),
            dma((SIDE,)), dma((SIDE,)), dma((SIDE, NC)), dma((NC, SIDE)),
        ],
        compiler_params=pltpu.CompilerParams(
            collective_id=0, has_side_effects=True, vmem_limit_bytes=63 * 2**20),
    )(train_acts, train_grads, query_acts, query_grads, basis_acts, basis_grads, eigenvalues,
      block_table.T, seq_lengths)


def solution(mesh):
    in_specs = (
        P(("seq", "blk"), None),
        P(("seq", "blk"), None),
        P(),
        P(),
        P("blk", "seq", None),
        P("blk", "seq", None),
        P("blk", "seq", None),
        P("blk", "seq", None),
        P("blk", "seq", None),
    )
    return jax.shard_map(
        on_device, mesh=mesh, in_specs=in_specs, out_specs=P(None, ("seq", "blk")),
        check_vma=False)
```

```python
import jax
import jax.numpy as jnp
from jax import lax
from jax.experimental import pallas as pl
from jax.experimental.pallas import tpu as pltpu
from jax.sharding import PartitionSpec as P

BLOCK = 256
SEQ_LEN = 1024
QUERIES = 8
QTOK = 32
DAMPING = 0.1
MESH = pl.DeviceIdType.MESH

SIDE = 4
NC = 2
NB = SIDE * SIDE * NC
NZ = 16
SHARD = 16
TOK = 128


def wrap(i, n=SIDE):
    return lax.rem(i + n, n)


def blk_of(y, x, core):
    return (wrap(y) * SIDE + wrap(x)) * NC + core


def dot(lhs, rhs, dims):
    return lax.dot_general(lhs, rhs, (dims, ((), ())), preferred_element_type=jnp.float32)


def kernel(
    acts_hbm, grads_hbm, qa_hbm, qg_hbm, ba_hbm, bg_hbm, eig_hbm, table, lengths,
    out_ref,
    acts, grads, eig, raw, send, recv, weights, act_t, grad_t, right, scores, home,
    load_sem, shard_sem, send_sem, recv_sem, up_sem, swap_sem, ring_sem,
    spread_sem, held_sem, back_sem, home_sem,
):
    z = lax.axis_index("seq")
    b = lax.axis_index("blk")
    core = lax.rem(b, NC)
    chip = lax.div(b, NC)
    y, x = lax.div(chip, SIDE), lax.rem(chip, SIDE)

    twist = 2 * lax.rem(z, 2)

    def holder(kind, j):
        if j == 2:
            return (wrap(z + (1 if kind == 0 else NZ - 1), NZ), blk_of(y, x, kind))
        return (z, blk_of(y + j, x, 0) if kind == 0 else blk_of(y, x + j, 1))

    def pair(kind, j, h):
        if kind == 0:
            return blk_of(wrap(y + j + twist), x + h, 0)
        return blk_of(y + h, wrap(x + j + twist), 1)

    def source(j, c):
        far = j == 2
        plane = jnp.where(far, wrap(z + jnp.where(core == 0, NZ - 1, 1), NZ), z)
        step = jnp.where(far, 0, SIDE - j)
        return (plane, jnp.where(core == 0, blk_of(y + step, x, c), blk_of(y, x + step, c)))

    def fellow(h):
        return (z, jnp.where(core == 0, blk_of(y, x - h, 0), blk_of(y - h, x, 1)))

    def beside():
        return jnp.where(core == 0, blk_of(y + 2, x, 0), blk_of(y, x + 2, 1))

    def column(to):
        return (wrap(z + to, NZ), beside() if to % 2 else b)

    shards = [
        pltpu.make_async_copy(
            hbm.at[0], raw.at[pl.ds(place * SHARD, SHARD)], shard_sem.at[place])
        for place, hbm in enumerate((ba_hbm, bg_hbm, qa_hbm, qg_hbm))
    ] + [pltpu.make_async_copy(eig_hbm.at[0], eig, shard_sem.at[4])]
    for copy in shards:
        copy.start()
    barrier = pltpu.get_barrier_semaphore()
    greeted = [(z, blk_of(y, x, 1 - core))]
    for j in range(1, SIDE):
        for c in range(NC):
            greeted += [(z, blk_of(y + j, x, c)), (z, blk_of(y, x + j, c))]
    for step in (2, 4, 8, NZ - 4, NZ - 2):
        greeted.append((wrap(z + step, NZ), b))
    for step in (1, NZ - 1):
        greeted.append((wrap(z + step, NZ), beside()))
        for c in range(NC):
            greeted.append((wrap(z + step, NZ), blk_of(y, x, c)))
    for peer in greeted:
        pl.semaphore_signal(barrier, inc=1, device_id=peer, device_id_type=MESH)

    for hbm, blocks, sem in ((acts_hbm, acts, 0), (grads_hbm, grads, 1)):

        @pl.loop(0, blocks.shape[0])
        def _(block):
            columns = pl.ds(pl.multiple_of(block * BLOCK, BLOCK), BLOCK)
            pltpu.make_async_copy(hbm.at[:, columns], blocks.at[block], load_sem.at[sem]).start()

    for copy in shards:
        copy.wait()
    raw[4 * SHARD : 5 * SHARD] = (eig[...] + DAMPING).astype(jnp.bfloat16)
    pl.semaphore_wait(barrier, len(greeted))

    def piece_copy(slot, to):
        piece = weights.at[0, slot]
        return pltpu.make_async_remote_copy(
            piece, piece, up_sem.at[0], ring_sem.at[slot],
            device_id=column(to), device_id_type=MESH)

    def arrived(step):
        slot = wrap(z + step, NZ)
        piece_copy(slot, 1).wait_recv()
        return slot

    def spread_copy(piece, h):
        return pltpu.make_async_remote_copy(
            weights.at[0, piece], weights.at[h, piece], spread_sem.at[h], held_sem.at[h],
            device_id=fellow(h), device_id_type=MESH)

    def spread(slot):
        for h in (1, 3):
            spread_copy(slot, h).start()

    swap = pltpu.make_async_remote_copy(
        raw, weights.at[0, z], swap_sem.at[0], ring_sem.at[z],
        device_id=(z, beside()), device_id_type=MESH)

    def token_copy(kind, j, h):
        return pltpu.make_async_remote_copy(
            send.at[h, kind, j], recv.at[h, j, core], send_sem.at[h, kind, j],
            recv_sem.at[h, j, core], device_id=holder(kind, j), device_id_type=MESH)

    def dispatch(h, offsets):
        for j in offsets:
            for kind in range(NC):
                owner = pair(kind, j, h)
                act_sel, grad_sel = acts[table[1, owner]], grads[table[0, owner]]

                def to_peer():
                    send[h, kind, j, :, 0:BLOCK] = act_sel
                    send[h, kind, j, :, BLOCK : 2 * BLOCK] = grad_sel
                    token_copy(kind, j, h).start()

                def to_self():
                    recv[h, 0, core, :, 0:BLOCK] = act_sel
                    recv[h, 0, core, :, BLOCK : 2 * BLOCK] = grad_sel

                if j == 0:
                    pl.when(core != kind)(to_peer)
                    pl.when(core == kind)(to_self)
                else:
                    to_peer()

    def hand_on(slot, steps):
        for to in steps:
            piece_copy(slot, to).start()
        spread(slot)

    @pl.when(twist > 0)
    def _():
        swap.start()
        swap.wait()

    @pl.when(twist == 0)
    def _():
        weights[0, z] = raw[...]

    hand_on(z, (4, NZ - 4, 8, 1, NZ - 1, 2, NZ - 2))
    for blocks, sem in ((acts, 0), (grads, 1)):
        pltpu.make_async_copy(blocks, blocks, load_sem.at[sem]).wait()
    dispatch(0, (0, 1, 3))
    dispatch(1, (0, 1, 3))
    for step in (4, NZ - 4):
        hand_on(arrived(step), (1, NZ - 1))
    hand_on(arrived(8), (1, NZ - 1, 2, NZ - 2))
    dispatch(0, (2,))
    dispatch(1, (2,))
    dispatch(3, (0, 1, 3))
    for step in (1, NZ - 1, 2, NZ - 2):
        spread(arrived(step))
    dispatch(3, (2,))
    dispatch(2, (0, 1, 3, 2))
    for step in (5, 13, 3, 11, 9, 7, 10, 6):
        spread(arrived(step))
    every = pl.ds(0, NZ)
    spread_copy(every, 2).start()

    def prepare(h):
        def gathered(place):
            rows = weights[h, :, place * SHARD : (place + 1) * SHARD, :]
            return rows.reshape(BLOCK, BLOCK)

        basis_act, basis_grad = gathered(0), gathered(1)
        act_t[...] = basis_act.astype(jnp.float32).T.astype(jnp.bfloat16)
        grad_t[...] = basis_grad.astype(jnp.float32).T.astype(jnp.bfloat16)
        qrot_acts = dot(gathered(2), basis_act, ((1,), (0,))).astype(jnp.bfloat16)
        qrot_grads = dot(gathered(3), basis_grad, ((1,), (0,))).astype(jnp.bfloat16)
        scale = 1.0 / (gathered(4).astype(jnp.float32) * QTOK)
        for q in range(QUERIES):
            rows = slice(q * QTOK, (q + 1) * QTOK)
            outer = dot(qrot_grads[rows], qrot_acts[rows], ((0,), (0,)))
            right[q * BLOCK : (q + 1) * BLOCK, :] = (outer * scale).astype(jnp.bfloat16)

    def return_copy(j, c):
        return pltpu.make_async_remote_copy(
            scores.at[j, c], home.at[core, j], back_sem.at[j, c], home_sem.at[core, j],
            device_id=source(j, c), device_id_type=MESH)

    def is_self(j, c):
        return jnp.logical_and(j == 0, c == core)

    @pl.loop(0, SIDE)
    def _(turn):
        h = lax.rem(turn * (turn + 1) // 2, SIDE)

        @pl.when(h > 0)
        def _():
            spread_copy(every, h).wait_recv()

        prepare(h)

        @pl.loop(0, SIDE)
        def _(place):
            j = lax.rem(2 + 3 * place, SIDE)
            for c in range(NC):

                @pl.when(jnp.logical_not(is_self(j, c)))
                def _():
                    pltpu.make_async_remote_copy(
                        send.at[h, 0, j], recv.at[h, j, c], send_sem.at[h, 0, j],
                        recv_sem.at[h, j, c], device_id=source(j, c),
                        device_id_type=MESH).wait_recv()

            tokens = recv[h, j].reshape(NC * TOK, 2 * BLOCK)
            rot_acts = dot(act_t[...], tokens[:, 0:BLOCK], ((1,), (1,))).astype(jnp.bfloat16)
            rot_grads = dot(grad_t[...], tokens[:, BLOCK:], ((1,), (1,))).astype(jnp.bfloat16)
            rot_grads = rot_grads.astype(jnp.float32)
            parts = []
            for q in range(QUERIES):
                mixed = dot(right[q * BLOCK : (q + 1) * BLOCK, :], rot_acts, ((1,), (0,)))
                parts.append(jnp.sum(mixed * rot_grads, axis=0, keepdims=True))
            score = jnp.concatenate(parts, axis=0)
            for c in range(NC):
                part = score[:, c * TOK : (c + 1) * TOK]

                @pl.when(turn == 0)
                def _():
                    scores[j, c] = part

                @pl.when(turn > 0)
                def _():
                    scores[j, c] = scores[j, c] + part

                @pl.when(jnp.logical_and(turn == SIDE - 1, jnp.logical_not(is_self(j, c))))
                def _():
                    return_copy(j, c).start()

    home[core, 0] = scores[0, core]
    for kind in range(NC):
        for j in range(SIDE):

            def wait_home():
                pltpu.make_async_remote_copy(
                    scores.at[j, 0], home.at[kind, j], back_sem.at[j, 0], home_sem.at[kind, j],
                    device_id=holder(kind, j), device_id_type=MESH).wait_recv()

            if j == 0:
                pl.when(core != kind)(wait_home)
            else:
                wait_home()

    total = home[0, 0]
    for kind in range(NC):
        for j in range(SIDE):
            if kind + j > 0:
                total = total + home[kind, j]
    base = (z * NB + b) * TOK
    place = lax.rem(base, SEQ_LEN) + lax.broadcasted_iota(jnp.int32, (QUERIES, TOK), 1)
    out_ref[...] = jnp.where(place < lengths[lax.div(base, SEQ_LEN)], total, 0.0)

    for j in range(SIDE):
        for kind in range(NC):

            def wait_sent():
                @pl.loop(0, SIDE)
                def _(h):
                    token_copy(kind, j, h).wait_send()

                return_copy(j, kind).wait_send()

            if j == 0:
                pl.when(core != kind)(wait_sent)
            else:
                wait_sent()

    gone = weights.at[0, pl.ds(0, NZ - 1)]
    pltpu.make_async_remote_copy(
        gone, gone, up_sem.at[0], ring_sem.at[0], device_id=(wrap(z + 1, NZ), b),
        device_id_type=MESH).wait_send()
    for h in range(1, SIDE):
        spread_copy(every, h).wait_send()


def on_device(
    train_acts, train_grads, block_table, seq_lengths,
    query_acts, query_grads, basis_acts, basis_grads, eigenvalues,
):
    bf16, f32 = jnp.bfloat16, jnp.float32
    vmem = pl.BlockSpec(memory_space=pltpu.VMEM)
    smem = pl.BlockSpec(memory_space=pltpu.SMEM)
    hbm = pl.BlockSpec(memory_space=pltpu.HBM)
    dma = pltpu.SemaphoreType.DMA
    return pl.pallas_call(
        kernel,
        out_shape=jax.ShapeDtypeStruct((QUERIES, TOK), f32),
        in_specs=[hbm] * 7 + [smem, smem],
        out_specs=vmem,
        scratch_shapes=[
            pltpu.VMEM((train_acts.shape[1] // BLOCK, TOK, BLOCK), bf16),
            pltpu.VMEM((train_grads.shape[1] // BLOCK, TOK, BLOCK), bf16),
            pltpu.VMEM((SHARD, BLOCK), f32),
            pltpu.VMEM((5 * SHARD, BLOCK), bf16),
            pltpu.VMEM((SIDE, NC, SIDE, TOK, 2 * BLOCK), bf16),
            pltpu.VMEM((SIDE, SIDE, NC, TOK, 2 * BLOCK), bf16),
            pltpu.VMEM((SIDE, NZ, 5 * SHARD, BLOCK), bf16),
            pltpu.VMEM((BLOCK, BLOCK), bf16),
            pltpu.VMEM((BLOCK, BLOCK), bf16),
            pltpu.VMEM((QUERIES * BLOCK, BLOCK), bf16),
            pltpu.VMEM((SIDE, NC, QUERIES, TOK), f32),
            pltpu.VMEM((NC, SIDE, QUERIES, TOK), f32),
            dma((2,)), dma((5,)), dma((SIDE, NC, SIDE)), dma((SIDE, SIDE, NC)),
            dma((1,)), dma((1,)), dma((NZ,)),
            dma((SIDE,)), dma((SIDE,)), dma((SIDE, NC)), dma((NC, SIDE)),
        ],
        compiler_params=pltpu.CompilerParams(
            collective_id=0, has_side_effects=True, vmem_limit_bytes=63 * 2**20),
    )(train_acts, train_grads, query_acts, query_grads, basis_acts, basis_grads, eigenvalues,
      block_table.T, seq_lengths)


def solution(mesh):
    in_specs = (
        P(("seq", "blk"), None),
        P(("seq", "blk"), None),
        P(),
        P(),
        P("blk", "seq", None),
        P("blk", "seq", None),
        P("blk", "seq", None),
        P("blk", "seq", None),
        P("blk", "seq", None),
    )
    return jax.shard_map(
        on_device, mesh=mesh, in_specs=in_specs, out_specs=P(None, ("seq", "blk")),
        check_vma=False)
```

```python
import jax
import jax.numpy as jnp
from jax import lax
from jax.experimental import pallas as pl
from jax.experimental.pallas import tpu as pltpu
from jax.sharding import PartitionSpec as P

BLOCK = 256
SEQ_LEN = 1024
QUERIES = 8
QTOK = 32
DAMPING = 0.1
MESH = pl.DeviceIdType.MESH

SIDE = 4
NC = 2
NB = SIDE * SIDE * NC
NZ = 16
SHARD = 16
TOK = 128


def wrap(i, n=SIDE):
    return lax.rem(i + n, n)


def blk_of(y, x, core):
    return (wrap(y) * SIDE + wrap(x)) * NC + core


def dot(lhs, rhs, dims):
    return lax.dot_general(lhs, rhs, (dims, ((), ())), preferred_element_type=jnp.float32)


def kernel(
    acts_hbm, grads_hbm, qa_hbm, qg_hbm, ba_hbm, bg_hbm, eig_hbm, table, lengths,
    out_ref,
    acts, grads, eig, raw, send, recv, weights, act_t, grad_t, right, scores, home,
    load_sem, shard_sem, send_sem, recv_sem, up_sem, swap_sem, ring_sem,
    spread_sem, held_sem, back_sem, home_sem,
):
    z = lax.axis_index("seq")
    b = lax.axis_index("blk")
    core = lax.rem(b, NC)
    chip = lax.div(b, NC)
    y, x = lax.div(chip, SIDE), lax.rem(chip, SIDE)

    twist = 2 * lax.rem(z, 2)

    def holder(kind, j):
        if j == 2:
            return (wrap(z + (1 if kind == 0 else NZ - 1), NZ), blk_of(y, x, kind))
        return (z, blk_of(y + j, x, 0) if kind == 0 else blk_of(y, x + j, 1))

    def pair(kind, j, h):
        if kind == 0:
            return blk_of(wrap(y + j + twist), x + h, 0)
        return blk_of(y + h, wrap(x + j + twist), 1)

    def source(j, c):
        far = j == 2
        plane = jnp.where(far, wrap(z + jnp.where(core == 0, NZ - 1, 1), NZ), z)
        step = jnp.where(far, 0, SIDE - j)
        return (plane, jnp.where(core == 0, blk_of(y + step, x, c), blk_of(y, x + step, c)))

    def fellow(h):
        return (z, jnp.where(core == 0, blk_of(y, x - h, 0), blk_of(y - h, x, 1)))

    def beside():
        return jnp.where(core == 0, blk_of(y + 2, x, 0), blk_of(y, x + 2, 1))

    def column(to):
        return (wrap(z + to, NZ), beside() if to % 2 else b)

    shards = [
        pltpu.make_async_copy(
            hbm.at[0], raw.at[pl.ds(place * SHARD, SHARD)], shard_sem.at[place])
        for place, hbm in enumerate((ba_hbm, bg_hbm, qa_hbm, qg_hbm))
    ] + [pltpu.make_async_copy(eig_hbm.at[0], eig, shard_sem.at[4])]
    for copy in shards:
        copy.start()
    barrier = pltpu.get_barrier_semaphore()
    greeted = [(z, blk_of(y, x, 1 - core))]
    for j in range(1, SIDE):
        for c in range(NC):
            greeted += [(z, blk_of(y + j, x, c)), (z, blk_of(y, x + j, c))]
    for step in (2, 4, 8, NZ - 4, NZ - 2):
        greeted.append((wrap(z + step, NZ), b))
    for step in (1, NZ - 1):
        greeted.append((wrap(z + step, NZ), beside()))
        for c in range(NC):
            greeted.append((wrap(z + step, NZ), blk_of(y, x, c)))
    for peer in greeted:
        pl.semaphore_signal(barrier, inc=1, device_id=peer, device_id_type=MESH)

    for hbm, blocks, sem in ((acts_hbm, acts, 0), (grads_hbm, grads, 1)):

        @pl.loop(0, blocks.shape[0])
        def _(block):
            columns = pl.ds(pl.multiple_of(block * BLOCK, BLOCK), BLOCK)
            pltpu.make_async_copy(hbm.at[:, columns], blocks.at[block], load_sem.at[sem]).start()

    for copy in shards:
        copy.wait()
    raw[4 * SHARD : 5 * SHARD] = (eig[...] + DAMPING).astype(jnp.bfloat16)
    pl.semaphore_wait(barrier, len(greeted))

    def piece_copy(slot, to):
        piece = weights.at[0, slot]
        return pltpu.make_async_remote_copy(
            piece, piece, up_sem.at[0], ring_sem.at[slot],
            device_id=column(to), device_id_type=MESH)

    def arrived(step):
        slot = wrap(z + step, NZ)
        piece_copy(slot, 1).wait_recv()
        return slot

    def spread_copy(piece, h):
        return pltpu.make_async_remote_copy(
            weights.at[0, piece], weights.at[h, piece], spread_sem.at[h], held_sem.at[h],
            device_id=fellow(h), device_id_type=MESH)

    def spread(slot):
        for h in (1, 3):
            spread_copy(slot, h).start()

    swap = pltpu.make_async_remote_copy(
        raw, weights.at[0, z], swap_sem.at[0], ring_sem.at[z],
        device_id=(z, beside()), device_id_type=MESH)

    def token_copy(kind, j, h):
        return pltpu.make_async_remote_copy(
            send.at[h, kind, j], recv.at[h, j, core], send_sem.at[h, kind, j],
            recv_sem.at[h, j, core], device_id=holder(kind, j), device_id_type=MESH)

    def dispatch(h, offsets):
        for j in offsets:
            for kind in range(NC):
                owner = pair(kind, j, h)
                act_sel, grad_sel = acts[table[1, owner]], grads[table[0, owner]]

                def to_peer():
                    send[h, kind, j, :, 0:BLOCK] = act_sel
                    send[h, kind, j, :, BLOCK : 2 * BLOCK] = grad_sel
                    token_copy(kind, j, h).start()

                def to_self():
                    recv[h, 0, core, :, 0:BLOCK] = act_sel
                    recv[h, 0, core, :, BLOCK : 2 * BLOCK] = grad_sel

                if j == 0:
                    pl.when(core != kind)(to_peer)
                    pl.when(core == kind)(to_self)
                else:
                    to_peer()

    def hand_on(slot, steps):
        for to in steps:
            piece_copy(slot, to).start()
        spread(slot)

    @pl.when(twist > 0)
    def _():
        swap.start()
        swap.wait()

    @pl.when(twist == 0)
    def _():
        weights[0, z] = raw[...]

    hand_on(z, (4, NZ - 4, 8, 1, NZ - 1, 2, NZ - 2))
    for blocks, sem in ((acts, 0), (grads, 1)):
        pltpu.make_async_copy(blocks, blocks, load_sem.at[sem]).wait()
    dispatch(0, (0, 1, 3))
    dispatch(1, (0, 1, 3))
    dispatch(3, (0, 1, 3))
    for step in (4, NZ - 4):
        hand_on(arrived(step), (1, NZ - 1))
    hand_on(arrived(8), (1, NZ - 1, 2, NZ - 2))
    dispatch(0, (2,))
    dispatch(1, (2,))
    for step in (1, NZ - 1, 2, NZ - 2):
        spread(arrived(step))
    dispatch(3, (2,))
    dispatch(2, (0, 1, 3, 2))
    for step in (5, 13, 3, 11, 9, 7, 10, 6):
        spread(arrived(step))
    every = pl.ds(0, NZ)
    spread_copy(every, 2).start()

    def prepare(h):
        def gathered(place):
            rows = weights[h, :, place * SHARD : (place + 1) * SHARD, :]
            return rows.reshape(BLOCK, BLOCK)

        basis_act, basis_grad = gathered(0), gathered(1)
        act_t[...] = basis_act.astype(jnp.float32).T.astype(jnp.bfloat16)
        grad_t[...] = basis_grad.astype(jnp.float32).T.astype(jnp.bfloat16)
        qrot_acts = dot(gathered(2), basis_act, ((1,), (0,))).astype(jnp.bfloat16)
        qrot_grads = dot(gathered(3), basis_grad, ((1,), (0,))).astype(jnp.bfloat16)
        scale = 1.0 / (gathered(4).astype(jnp.float32) * QTOK)
        for q in range(QUERIES):
            rows = slice(q * QTOK, (q + 1) * QTOK)
            outer = dot(qrot_grads[rows], qrot_acts[rows], ((0,), (0,)))
            right[q * BLOCK : (q + 1) * BLOCK, :] = (outer * scale).astype(jnp.bfloat16)

    def return_copy(j, c):
        return pltpu.make_async_remote_copy(
            scores.at[j, c], home.at[core, j], back_sem.at[j, c], home_sem.at[core, j],
            device_id=source(j, c), device_id_type=MESH)

    def is_self(j, c):
        return jnp.logical_and(j == 0, c == core)

    @pl.loop(0, SIDE)
    def _(turn):
        h = lax.rem(turn * (turn + 1) // 2, SIDE)

        @pl.when(h > 0)
        def _():
            spread_copy(every, h).wait_recv()

        prepare(h)

        @pl.loop(0, SIDE)
        def _(place):
            j = lax.rem(2 + 3 * place, SIDE)
            for c in range(NC):

                @pl.when(jnp.logical_not(is_self(j, c)))
                def _():
                    pltpu.make_async_remote_copy(
                        send.at[h, 0, j], recv.at[h, j, c], send_sem.at[h, 0, j],
                        recv_sem.at[h, j, c], device_id=source(j, c),
                        device_id_type=MESH).wait_recv()

            tokens = recv[h, j].reshape(NC * TOK, 2 * BLOCK)
            rot_acts = dot(act_t[...], tokens[:, 0:BLOCK], ((1,), (1,))).astype(jnp.bfloat16)
            rot_grads = dot(grad_t[...], tokens[:, BLOCK:], ((1,), (1,))).astype(jnp.bfloat16)
            rot_grads = rot_grads.astype(jnp.float32)
            parts = []
            for q in range(QUERIES):
                mixed = dot(right[q * BLOCK : (q + 1) * BLOCK, :], rot_acts, ((1,), (0,)))
                parts.append(jnp.sum(mixed * rot_grads, axis=0, keepdims=True))
            score = jnp.concatenate(parts, axis=0)
            for c in range(NC):
                part = score[:, c * TOK : (c + 1) * TOK]

                @pl.when(turn == 0)
                def _():
                    scores[j, c] = part

                @pl.when(turn > 0)
                def _():
                    scores[j, c] = scores[j, c] + part

                @pl.when(jnp.logical_and(turn == SIDE - 1, jnp.logical_not(is_self(j, c))))
                def _():
                    return_copy(j, c).start()

    home[core, 0] = scores[0, core]
    for kind in range(NC):
        for j in range(SIDE):

            def wait_home():
                pltpu.make_async_remote_copy(
                    scores.at[j, 0], home.at[kind, j], back_sem.at[j, 0], home_sem.at[kind, j],
                    device_id=holder(kind, j), device_id_type=MESH).wait_recv()

            if j == 0:
                pl.when(core != kind)(wait_home)
            else:
                wait_home()

    total = home[0, 0]
    for kind in range(NC):
        for j in range(SIDE):
            if kind + j > 0:
                total = total + home[kind, j]
    base = (z * NB + b) * TOK
    place = lax.rem(base, SEQ_LEN) + lax.broadcasted_iota(jnp.int32, (QUERIES, TOK), 1)
    out_ref[...] = jnp.where(place < lengths[lax.div(base, SEQ_LEN)], total, 0.0)

    for j in range(SIDE):
        for kind in range(NC):

            def wait_sent():
                @pl.loop(0, SIDE)
                def _(h):
                    token_copy(kind, j, h).wait_send()

                return_copy(j, kind).wait_send()

            if j == 0:
                pl.when(core != kind)(wait_sent)
            else:
                wait_sent()

    gone = weights.at[0, pl.ds(0, NZ - 1)]
    pltpu.make_async_remote_copy(
        gone, gone, up_sem.at[0], ring_sem.at[0], device_id=(wrap(z + 1, NZ), b),
        device_id_type=MESH).wait_send()
    for h in range(1, SIDE):
        spread_copy(every, h).wait_send()


def on_device(
    train_acts, train_grads, block_table, seq_lengths,
    query_acts, query_grads, basis_acts, basis_grads, eigenvalues,
):
    bf16, f32 = jnp.bfloat16, jnp.float32
    vmem = pl.BlockSpec(memory_space=pltpu.VMEM)
    smem = pl.BlockSpec(memory_space=pltpu.SMEM)
    hbm = pl.BlockSpec(memory_space=pltpu.HBM)
    dma = pltpu.SemaphoreType.DMA
    return pl.pallas_call(
        kernel,
        out_shape=jax.ShapeDtypeStruct((QUERIES, TOK), f32),
        in_specs=[hbm] * 7 + [smem, smem],
        out_specs=vmem,
        scratch_shapes=[
            pltpu.VMEM((train_acts.shape[1] // BLOCK, TOK, BLOCK), bf16),
            pltpu.VMEM((train_grads.shape[1] // BLOCK, TOK, BLOCK), bf16),
            pltpu.VMEM((SHARD, BLOCK), f32),
            pltpu.VMEM((5 * SHARD, BLOCK), bf16),
            pltpu.VMEM((SIDE, NC, SIDE, TOK, 2 * BLOCK), bf16),
            pltpu.VMEM((SIDE, SIDE, NC, TOK, 2 * BLOCK), bf16),
            pltpu.VMEM((SIDE, NZ, 5 * SHARD, BLOCK), bf16),
            pltpu.VMEM((BLOCK, BLOCK), bf16),
            pltpu.VMEM((BLOCK, BLOCK), bf16),
            pltpu.VMEM((QUERIES * BLOCK, BLOCK), bf16),
            pltpu.VMEM((SIDE, NC, QUERIES, TOK), f32),
            pltpu.VMEM((NC, SIDE, QUERIES, TOK), f32),
            dma((2,)), dma((5,)), dma((SIDE, NC, SIDE)), dma((SIDE, SIDE, NC)),
            dma((1,)), dma((1,)), dma((NZ,)),
            dma((SIDE,)), dma((SIDE,)), dma((SIDE, NC)), dma((NC, SIDE)),
        ],
        compiler_params=pltpu.CompilerParams(
            collective_id=0, has_side_effects=True, vmem_limit_bytes=63 * 2**20),
    )(train_acts, train_grads, query_acts, query_grads, basis_acts, basis_grads, eigenvalues,
      block_table.T, seq_lengths)


def solution(mesh):
    in_specs = (
        P(("seq", "blk"), None),
        P(("seq", "blk"), None),
        P(),
        P(),
        P("blk", "seq", None),
        P("blk", "seq", None),
        P("blk", "seq", None),
        P("blk", "seq", None),
        P("blk", "seq", None),
    )
    return jax.shard_map(
        on_device, mesh=mesh, in_specs=in_specs, out_specs=P(None, ("seq", "blk")),
        check_vma=False)
```
